128 devices in a mesh: layer: 4 (over x_hi, core), tok: 32 (over z, x_lo, y).
Axes of the slice: x: 4 (x_hi: 2, x_lo: 2; x = x_hi * 2 + x_lo), y: 4, z: 4, core: 2. Of those that a mesh axis runs over, the one named last changes fastest.
Arguments:
- kv_cache: bfloat16 [4, 2, 2, 1, 16384, 1024], P('layer', None, None, None, 'tok'), may hold values from -6 to 6
- keep_mask: int32 [4, 1, 16384], P('layer', None, 'tok'), may hold values 0 or 1
- lengths: int32 [1], replicated, may hold values from 4096 to 16384
Outputs:
- decode_cache: bfloat16 [1, 8, 8, 2, 16384, 128], P(None, 'layer', None, None, 'tok')
The draws below stay inside these ranges and needn't reach their ends.
Inputs may be any that keep to these rules, and one draw needn't show every extreme that they name: `keep_mask`: 1 keeps the token of both layers of the pair unmerged. `lengths`: positions at or past a sequence's length are padding.
All inputs are finite; a program needn't handle non-finite values. No bound on the sum of `keep_mask` on one device may be relied on, other than what follows from the above.
Results may differ from the reference program's by a relative error of at most 0.001.
Values may be sent and summed in bfloat16 or wider, within the bound.
A program may use at most 64 MiB of HBM per device.

```python
import jax
import jax.numpy as jnp
from jax import lax

KVH = 8
HD = 128
PAGE = 16
SEQS = 1
PAIRS = 4
LEN = 16384
N_TOK = 32


def touch_ends(array, rng, smallest, top_value):
    longest = array.shape.index(max(array.shape))
    spots = []
    for shift in (0, 1):
        where = [jax.random.randint(jax.random.fold_in(rng, axis), (), 0, length) for axis, length in enumerate(array.shape)]
        where[longest] = (where[longest] + shift) % array.shape[longest]
        spots.append(tuple(where))
    return array.at[spots[0]].set(smallest).at[spots[1]].set(top_value)


def level_of(rng, extent, cuts, smallest, largest):
    def one(dim, shards_of):
        heights = jax.random.uniform(jax.random.fold_in(jax.random.fold_in(rng, 6), dim), (shards_of,), jnp.float32, smallest / len(cuts), largest / len(cuts))
        return jnp.repeat(jnp.exp(heights), extent[dim] // shards_of).reshape((-1,) + (1,) * (len(extent) - dim - 1))

    level = one(*cuts[0])
    for cut in cuts[1:]:
        level = level * one(*cut)
    return level


def centred(stream_key, extent, scale, limit, shards=(), held_as=jnp.bfloat16):
    loudness = level_of(stream_key, extent, shards, -0.22, 0.18) if shards else 1.0
    entries = jax.random.normal(stream_key, extent, jnp.float32) * scale * loudness
    return jnp.minimum(jnp.maximum(entries, -limit), limit).astype(held_as)


def setup_inputs(seed: int = 0) -> dict:
    splits = jax.random.split(jax.random.key(seed), 4)
    kv_cache = centred(splits[0], (PAIRS, 2, 2, SEQS, LEN, KVH * HD), 1.0, 6.0, ((0, 4), (4, 32)))
    keep_mask = touch_ends((jax.random.randint(splits[1], (PAIRS, SEQS, LEN), 0, 8) < 1).astype(jnp.int32), jax.random.fold_in(splits[1], 1), 0, 1)
    lengths = jax.random.randint(splits[2], (SEQS,), LEN // 4, LEN + 1).astype(jnp.int32)
    return {"kv_cache": kv_cache, "keep_mask": keep_mask, "lengths": lengths}


epsilon = 1e-06

def merge_pair(lower_layer, upper_layer, retained, inside):
    lower_scale = jnp.sqrt(lax.optimization_barrier(jnp.mean(lower_layer * lower_layer, axis=-1, keepdims=True)) + epsilon)
    upper_scale = jnp.sqrt(lax.optimization_barrier(jnp.mean(upper_layer * upper_layer, axis=-1, keepdims=True)) + epsilon)
    summed = lower_layer / lower_scale + upper_layer / upper_scale
    direction = summed / jnp.sqrt(lax.optimization_barrier(jnp.mean(summed * summed, axis=-1, keepdims=True)) + epsilon)
    lower_out = jnp.where(retained, lower_layer, lower_scale * direction)
    upper_out = jnp.where(retained, upper_layer, upper_scale * direction)
    lower_out = jnp.where(inside, lower_out, jnp.zeros_like(lower_out))
    upper_out = jnp.where(inside, upper_out, jnp.zeros_like(upper_out))
    return jnp.stack([lower_out, upper_out], axis=0).astype(jnp.bfloat16)

def reference(kv_cache, keep_mask, lengths):
    position = jnp.arange(LEN, dtype=jnp.int32)
    inside = (position[None, :] < lengths[:, None])[None, :, :, None, None]

    def one_pair(operands):
        pair_cache, pair_keep = operands
        values = pair_cache.astype(jnp.float32).reshape(2, 2, SEQS, LEN, KVH, HD)
        retained = (pair_keep > 0)[None, :, :, None, None]
        return merge_pair(values[0], values[1], retained, inside)
    merged = lax.map(one_pair, (kv_cache, keep_mask))
    rounds = LEN // (N_TOK * PAGE)
    merged = merged.reshape(PAIRS, 2, 2, SEQS, rounds, N_TOK, PAGE, KVH, HD)
    ordered = merged.transpose(3, 7, 0, 1, 2, 5, 4, 6, 8)
    return ordered.reshape(SEQS, KVH, 2 * PAIRS, 2, LEN, HD)
```

```python
import functools
import itertools

import jax
import jax.numpy as jnp
from jax import lax
from jax.experimental import pallas as pl
from jax.experimental.pallas import tpu as pltpu
from jax.sharding import PartitionSpec as P

KVH = 8
HD = 128
PAGE = 16
EPS = 1e-06
MESH = pl.DeviceIdType.MESH
CHUNKS = [(1, 1, 1), (0, 1, 1), (1, 0, 1), (1, 1, 0), (0, 0, 1), (0, 1, 0), (1, 0, 0), (0, 0, 0)]


def place():
    layer = lax.axis_index("layer")
    tok = lax.axis_index("tok")
    x = (layer // 2) * 2 + (tok // 4) % 2
    return layer, tok, x, tok % 4, tok // 8, layer % 2


def target(x, y, z, core):
    return (x // 2) * 2 + core, z * 8 + (x % 2) * 4 + y


def sends_of(chunk):
    px, py, pz = chunk
    out = []
    for dc in (0, 1):
        for sy, sz in ((0, 0), (0, 2), (2, 0), (2, 2)):
            o = (px, py + sy, pz + sz)
            n = (px + 2, (py + 2 - sy) if py else py + sy, (pz + 2 - sz) if pz else pz + sz)
            out += [o + (dc,), n + (dc,)]
    assert len(set(out)) == 16
    return out


def merge(in_v, keep_v, move_v, buf, k, at):
    zl, xl, yl = at
    def body(step, carry):
        h, c = step // 2, step % 2
        cols = pl.ds(pl.multiple_of(h * HD, HD), HD)
        a = in_v[k, 0, c, :, :, :, cols].reshape(64, HD).astype(jnp.float32)
        b = in_v[k, 1, c, :, :, :, cols].reshape(64, HD).astype(jnp.float32)
        keep = keep_v[:, zl, xl, :, yl].reshape(64, HD)
        move = move_v[:, zl, xl, :, yl].reshape(64, HD)
        ma = jnp.sum(a * a, axis=-1, keepdims=True) * (1.0 / HD) + EPS
        mb = jnp.sum(b * b, axis=-1, keepdims=True) * (1.0 / HD) + EPS
        ia, ib = lax.rsqrt(ma), lax.rsqrt(mb)
        u = a * ia + b * ib
        mu = jnp.sum(u * u, axis=-1, keepdims=True) * (1.0 / HD) + EPS
        s = move * lax.rsqrt(mu)
        lower = (keep * a + (s * (ma * ia)) * u).astype(jnp.bfloat16)
        upper = (keep * b + (s * (mb * ib)) * u).astype(jnp.bfloat16)
        for zh, yh in itertools.product(range(2), range(2)):
            first = (zh * 2 + yh) * PAGE
            block = (zh * 16 + zl * 8 + xl * 4 + yh * 2 + yl) * 4 + h // 2
            buf[block, h % 2, 0, c] = lower[first : first + PAGE]
            buf[block, h % 2, 1, c] = upper[first : first + PAGE]
        return carry

    lax.fori_loop(0, 2 * KVH, body, 0, unroll=2)


def kernel(len_ref, mask_ref, kv_ref, out_ref, in_v, keep_v, move_v, buf, load_sem, own_sem, send_sem, recv_sem):
    layer, tok, x, y, z, core = place()
    everyone = [o for o in itertools.product(range(4), range(4), range(4), range(2)) if any(o)]

    def to(o):
        return target((x + o[0]) % 4, (y + o[1]) % 4, (z + o[2]) % 4, (core + o[3]) % 2)

    def at(chunk):
        px, py, pz = chunk
        return (z + pz) % 2, (x + px) % 2, (y + py) % 2

    loads = []
    for k, chunk in enumerate(CHUNKS):
        zl, xl, yl = at(chunk)
        load = pltpu.make_async_copy(kv_ref.at[:, :, :, zl, xl, :, yl], in_v.at[k], load_sem.at[k])
        load.start()
        loads.append(load)

    barrier = pltpu.get_barrier_semaphore()
    for o in everyone:
        pl.semaphore_signal(barrier, inc=1, device_id=to(o), device_id_type=MESH)

    limit = len_ref[0]
    square = (128, 128)
    diagonal = lax.broadcasted_iota(jnp.int32, square, 0) == lax.broadcasted_iota(jnp.int32, square, 1)
    for k in range(4):
        mask = jnp.broadcast_to(mask_ref[:, k * 128 : (k + 1) * 128], square)
        kept = jnp.sum(jnp.where(diagonal & (mask > 0), 1.0, 0.0), axis=-1, keepdims=True)
        position = tok * 512 + k * 128 + lax.broadcasted_iota(jnp.int32, square, 0)
        inside = jnp.where(position < limit, 1.0, 0.0)
        keep_v[k // 2, k % 2] = (kept * inside).reshape(2, 2, 2, PAGE, HD)
        move_v[k // 2, k % 2] = ((1.0 - kept) * inside).reshape(2, 2, 2, PAGE, HD)

    slots = pl.ds(pl.multiple_of(tok * PAGE, PAGE), PAGE)
    here = out_ref.at[0, :, pl.ds(layer * 2, 2), :, slots, :]

    def block(o):
        there = to(o)
        return there, buf.at[there[1] * 4 + there[0]]

    def send(chunk):
        for o in sends_of(chunk):
            there, data = block(o)
            if any(o):
                pltpu.make_async_remote_copy(
                    src_ref=data, dst_ref=here, send_sem=send_sem, recv_sem=recv_sem,
                    device_id=there, device_id_type=MESH,
                ).start()
            else:
                pltpu.make_async_copy(data, here, own_sem).start()

    for k, chunk in enumerate(CHUNKS):
        loads[k].wait()
        merge(in_v, keep_v, move_v, buf, k, at(chunk))
        if k == 0:
            pl.semaphore_wait(barrier, len(everyone))
            send(chunk)
        if k > 1:
            send(CHUNKS[k - 1])
    send(CHUNKS[-1])

    pltpu.make_async_copy(block((0, 0, 0, 0))[1], here, own_sem).wait()
    rest = buf.at[pl.ds(0, 127)]
    pltpu.make_async_copy(rest, rest, send_sem).wait()
    pltpu.make_async_copy(rest, rest, recv_sem).wait()


def shards(kv_cache, keep_mask, lengths):
    return pl.pallas_call(
        kernel,
        out_shape=jax.ShapeDtypeStruct((1, 2, 8, 2, 512, HD), jnp.bfloat16),
        in_specs=[
            pl.BlockSpec(memory_space=pltpu.SMEM),
            pl.BlockSpec(memory_space=pltpu.VMEM),
            pl.BlockSpec(memory_space=pl.ANY),
        ],
        out_specs=pl.BlockSpec(memory_space=pl.ANY),
        scratch_shapes=[
            pltpu.VMEM((8, 2, 2, 2, 2, PAGE, KVH * HD), jnp.bfloat16),
            pltpu.VMEM((2, 2, 2, 2, 2, PAGE, HD), jnp.float32),
            pltpu.VMEM((2, 2, 2, 2, 2, PAGE, HD), jnp.float32),
            pltpu.VMEM((128, 2, 2, 2, PAGE, HD), jnp.bfloat16),
            pltpu.SemaphoreType.DMA((8,)),
            pltpu.SemaphoreType.DMA,
            pltpu.SemaphoreType.DMA,
            pltpu.SemaphoreType.DMA,
        ],
        compiler_params=pltpu.CompilerParams(collective_id=0, has_side_effects=True),
    )(lengths, keep_mask.reshape(1, 512), kv_cache.reshape(2, 2, 2, 2, 2, 2, 2, PAGE, KVH * HD))


def solution(mesh):
    in_specs = (P("layer", None, None, None, "tok", None), P("layer", None, "tok"), P())
    out_specs = P(None, "layer", None, None, "tok", None)
    return jax.shard_map(shards, mesh=mesh, in_specs=in_specs, out_specs=out_specs, check_vma=False)
```

```python
import functools
import itertools

import jax
import jax.numpy as jnp
from jax import lax
from jax.experimental import pallas as pl
from jax.experimental.pallas import tpu as pltpu
from jax.sharding import PartitionSpec as P

KVH = 8
HD = 128
PAGE = 16
EPS = 1e-06
MESH = pl.DeviceIdType.MESH
CHUNKS = [(1, 1, 1), (0, 0, 0), (0, 1, 1), (1, 0, 0), (1, 0, 1), (0, 1, 0), (1, 1, 0), (0, 0, 1)]


def place():
    layer = lax.axis_index("layer")
    tok = lax.axis_index("tok")
    x = (layer // 2) * 2 + (tok // 4) % 2
    return layer, tok, x, tok % 4, tok // 8, layer % 2


def target(x, y, z, core):
    return (x // 2) * 2 + core, z * 8 + (x % 2) * 4 + y


def sends_of(chunk):
    px, py, pz = chunk
    out = []
    for dc in (0, 1):
        for sy, sz in ((0, 0), (2, 2), (2, 0), (0, 2)):
            o = (px, py + sy, pz + sz)
            n = (px + 2, (py + 2 - sy) if py else py + sy, (pz + 2 - sz) if pz else pz + sz)
            out += [o + (dc,), n + (dc,)]
    assert len(set(out)) == 16
    return out


def merge(in_v, keep_v, move_v, buf, k, at):
    zl, xl, yl = at
    def body(step, carry):
        h, c = step // 2, step % 2
        cols = pl.ds(pl.multiple_of(h * HD, HD), HD)
        a = in_v[k, 0, c, :, :, :, cols].reshape(64, HD).astype(jnp.float32)
        b = in_v[k, 1, c, :, :, :, cols].reshape(64, HD).astype(jnp.float32)
        keep = keep_v[:, zl, xl, :, yl].reshape(64, HD)
        move = move_v[:, zl, xl, :, yl].reshape(64, HD)
        ma = jnp.sum(a * a, axis=-1, keepdims=True) * (1.0 / HD) + EPS
        mb = jnp.sum(b * b, axis=-1, keepdims=True) * (1.0 / HD) + EPS
        ia, ib = lax.rsqrt(ma), lax.rsqrt(mb)
        u = a * ia + b * ib
        mu = jnp.sum(u * u, axis=-1, keepdims=True) * (1.0 / HD) + EPS
        s = move * lax.rsqrt(mu)
        lower = (keep * a + (s * (ma * ia)) * u).astype(jnp.bfloat16)
        upper = (keep * b + (s * (mb * ib)) * u).astype(jnp.bfloat16)
        for zh, yh in itertools.product(range(2), range(2)):
            first = (zh * 2 + yh) * PAGE
            block = (zh * 16 + zl * 8 + xl * 4 + yh * 2 + yl) * 4 + h // 2
            buf[block, h % 2, 0, c] = lower[first : first + PAGE]
            buf[block, h % 2, 1, c] = upper[first : first + PAGE]
        return carry

    lax.fori_loop(0, 2 * KVH, body, 0, unroll=2)


def kernel(len_ref, mask_ref, kv_ref, out_ref, in_v, keep_v, move_v, buf, load_sem, own_sem, send_sem, recv_sem):
    layer, tok, x, y, z, core = place()
    everyone = [o for o in itertools.product(range(4), range(4), range(4), range(2)) if any(o)]

    def to(o):
        return target((x + o[0]) % 4, (y + o[1]) % 4, (z + o[2]) % 4, (core + o[3]) % 2)

    def at(chunk):
        px, py, pz = chunk
        return (z + pz) % 2, (x + px) % 2, (y + py) % 2

    loads = []
    for k, chunk in enumerate(CHUNKS):
        zl, xl, yl = at(chunk)
        load = pltpu.make_async_copy(kv_ref.at[:, :, :, zl, xl, :, yl], in_v.at[k], load_sem.at[k])
        load.start()
        loads.append(load)

    barrier = pltpu.get_barrier_semaphore()
    for o in everyone:
        pl.semaphore_signal(barrier, inc=1, device_id=to(o), device_id_type=MESH)

    limit = len_ref[0]
    square = (128, 128)
    diagonal = lax.broadcasted_iota(jnp.int32, square, 0) == lax.broadcasted_iota(jnp.int32, square, 1)
    for k in range(4):
        mask = jnp.broadcast_to(mask_ref[:, k * 128 : (k + 1) * 128], square)
        kept = jnp.sum(jnp.where(diagonal & (mask > 0), 1.0, 0.0), axis=-1, keepdims=True)
        position = tok * 512 + k * 128 + lax.broadcasted_iota(jnp.int32, square, 0)
        inside = jnp.where(position < limit, 1.0, 0.0)
        keep_v[k // 2, k % 2] = (kept * inside).reshape(2, 2, 2, PAGE, HD)
        move_v[k // 2, k % 2] = ((1.0 - kept) * inside).reshape(2, 2, 2, PAGE, HD)

    slots = pl.ds(pl.multiple_of(tok * PAGE, PAGE), PAGE)
    here = out_ref.at[0, :, pl.ds(layer * 2, 2), :, slots, :]

    def block(o):
        there = to(o)
        return there, buf.at[there[1] * 4 + there[0]]

    def send(chunk):
        for o in sends_of(chunk):
            there, data = block(o)
            if any(o):
                pltpu.make_async_remote_copy(
                    src_ref=data, dst_ref=here, send_sem=send_sem, recv_sem=recv_sem,
                    device_id=there, device_id_type=MESH,
                ).start()
            else:
                pltpu.make_async_copy(data, here, own_sem).start()

    for k, chunk in enumerate(CHUNKS):
        loads[k].wait()
        merge(in_v, keep_v, move_v, buf, k, at(chunk))
        if k == 0:
            pl.semaphore_wait(barrier, len(everyone))
            send(chunk)
        if k > 1:
            send(CHUNKS[k - 1])
    send(CHUNKS[-1])

    pltpu.make_async_copy(block((0, 0, 0, 0))[1], here, own_sem).wait()
    rest = buf.at[pl.ds(0, 127)]
    pltpu.make_async_copy(rest, rest, send_sem).wait()
    pltpu.make_async_copy(rest, rest, recv_sem).wait()


def put_out(in_ref, out_ref, sem):
    copies = []
    for h, j in itertools.product(range(2), range(8)):
        copies.append(pltpu.make_async_copy(in_ref.at[0, h, j], out_ref.at[0, h, j], sem.at[h * 8 + j]))
    for copy in copies:
        copy.start()
    for copy in copies:
        copy.wait()


def shards(kv_cache, keep_mask, lengths):
    landed = pl.pallas_call(
        kernel,
        out_shape=pltpu.VMEM((1, 2, 8, 2, 512, HD), jnp.bfloat16),
        in_specs=[
            pl.BlockSpec(memory_space=pltpu.SMEM),
            pl.BlockSpec(memory_space=pltpu.VMEM),
            pl.BlockSpec(memory_space=pltpu.HBM),
        ],
        out_specs=pl.BlockSpec(memory_space=pltpu.VMEM),
        scratch_shapes=[
            pltpu.VMEM((8, 2, 2, 2, 2, PAGE, KVH * HD), jnp.bfloat16),
            pltpu.VMEM((2, 2, 2, 2, 2, PAGE, HD), jnp.float32),
            pltpu.VMEM((2, 2, 2, 2, 2, PAGE, HD), jnp.float32),
            pltpu.VMEM((128, 2, 2, 2, PAGE, HD), jnp.bfloat16),
            pltpu.SemaphoreType.DMA((8,)),
            pltpu.SemaphoreType.DMA,
            pltpu.SemaphoreType.DMA,
            pltpu.SemaphoreType.DMA,
        ],
        compiler_params=pltpu.CompilerParams(collective_id=0, has_side_effects=True, vmem_limit_bytes=58 << 20),
    )(lengths, keep_mask.reshape(1, 512), kv_cache.reshape(2, 2, 2, 2, 2, 2, 2, PAGE, KVH * HD))
    return pl.pallas_call(
        put_out,
        out_shape=jax.ShapeDtypeStruct((1, 2, 8, 2, 512, HD), jnp.bfloat16),
        in_specs=[pl.BlockSpec(memory_space=pltpu.VMEM)],
        out_specs=pl.BlockSpec(memory_space=pl.ANY),
        scratch_shapes=[pltpu.SemaphoreType.DMA((16,))],
        compiler_params=pltpu.CompilerParams(vmem_limit_bytes=16 << 20),
    )(landed)


def solution(mesh):
    in_specs = (P("layer", None, None, None, "tok", None), P("layer", None, "tok"), P())
    out_specs = P(None, "layer", None, None, "tok", None)
    return jax.shard_map(shards, mesh=mesh, in_specs=in_specs, out_specs=out_specs, check_vma=False)
```

```python
import functools
import itertools

import jax
import jax.numpy as jnp
from jax import lax
from jax.experimental import pallas as pl
from jax.experimental.pallas import tpu as pltpu
from jax.sharding import PartitionSpec as P

KVH = 8
HD = 128
PAGE = 16
EPS = 1e-06
MESH = pl.DeviceIdType.MESH
CHUNKS = [(1, 1, 1), (0, 0, 0), (0, 1, 1), (1, 0, 0), (1, 0, 1), (0, 1, 0), (1, 1, 0), (0, 0, 1)]


def place():
    layer = lax.axis_index("layer")
    tok = lax.axis_index("tok")
    x = (layer // 2) * 2 + (tok // 4) % 2
    return layer, tok, x, tok % 4, tok // 8, layer % 2


def hops(o):
    return sum(min(v, 4 - v) for v in o[:3])


def sends_of(chunk):
    px, py, pz = chunk
    out = []
    for dc in (0, 1):
        for sy, sz in ((0, 0), (2, 2), (2, 0), (0, 2)):
            o = (px, py + sy, pz + sz)
            n = (px + 2, (py + 2 - sy) if py else py + sy, (pz + 2 - sz) if pz else pz + sz)
            out += [o + (dc,), n + (dc,)]
    assert len(set(out)) == 16
    return out


def merge(in_v, keep_v, move_v, buf, k, at):
    zl, xl, yl = at
    def body(step, carry):
        h, c = step // 2, step % 2
        cols = pl.ds(pl.multiple_of(h * HD, HD), HD)
        a = in_v[k, 0, c, :, :, :, cols].reshape(64, HD).astype(jnp.float32)
        b = in_v[k, 1, c, :, :, :, cols].reshape(64, HD).astype(jnp.float32)
        keep = keep_v[:, zl, xl, :, yl].reshape(64, HD)
        move = move_v[:, zl, xl, :, yl].reshape(64, HD)
        ma = jnp.sum(a * a, axis=-1, keepdims=True) * (1.0 / HD) + EPS
        mb = jnp.sum(b * b, axis=-1, keepdims=True) * (1.0 / HD) + EPS
        ia, ib = lax.rsqrt(ma), lax.rsqrt(mb)
        u = a * ia + b * ib
        mu = jnp.sum(u * u, axis=-1, keepdims=True) * (1.0 / HD) + EPS
        s = move * lax.rsqrt(mu)
        lower = (keep * a + (s * (ma * ia)) * u).astype(jnp.bfloat16)
        upper = (keep * b + (s * (mb * ib)) * u).astype(jnp.bfloat16)
        for zh, yh in itertools.product(range(2), range(2)):
            first = (zh * 2 + yh) * PAGE
            block = (zh * 16 + zl * 8 + xl * 4 + yh * 2 + yl) * 4 + h // 2
            buf[block, h % 2, 0, c] = lower[first : first + PAGE]
            buf[block, h % 2, 1, c] = upper[first : first + PAGE]
        return carry

    lax.fori_loop(0, 2 * KVH, body, 0, unroll=8)


def kernel(len_ref, mask_hbm, kv_ref, out_ref, mask_ref, in_v, keep_v, move_v, buf, load_sem, own_sem, send_sem, recv_sem):
    layer, tok, x, y, z, core = place()
    everyone = [o for o in itertools.product(range(4), range(4), range(4), range(2)) if any(o)]
    everyone = sorted(everyone, key=hops, reverse=True)

    xs, ys, zs = ([lax.rem(v + d, 4) for d in range(4)] for v in (x, y, z))
    cores = [core, 1 - core]
    to_layer = [[lax.div(v, 2) * 2 + c for c in cores] for v in xs]
    to_xy = [[lax.rem(v, 2) * 4 + w for w in ys] for v in xs]

    def to(o):
        dx, dy, dz, dc = o
        return to_layer[dx][dc], zs[dz] * 8 + to_xy[dx][dy]

    def at(chunk):
        px, py, pz = chunk
        return (z + pz) % 2, (x + px) % 2, (y + py) % 2

    loads = []
    for k, chunk in enumerate(CHUNKS):
        zl, xl, yl = at(chunk)
        loads.append(pltpu.make_async_copy(kv_ref.at[:, :, :, zl, xl, :, yl], in_v.at[k], load_sem.at[k]))
    get_mask = pltpu.make_async_copy(mask_hbm, mask_ref, load_sem.at[9])
    get_mask.start()
    loads[0].start()

    barrier = pltpu.get_barrier_semaphore()
    for o in everyone:
        pl.semaphore_signal(barrier, inc=1, device_id=to(o), device_id_type=MESH)
    for load in loads[1:]:
        load.start()

    get_mask.wait()
    limit = len_ref[0]
    square = (128, 128)
    diagonal = lax.broadcasted_iota(jnp.int32, square, 0) == lax.broadcasted_iota(jnp.int32, square, 1)
    for k in range(4):
        mask = jnp.broadcast_to(mask_ref[:, k * 128 : (k + 1) * 128], square)
        kept = jnp.sum(jnp.where(diagonal & (mask > 0), 1.0, 0.0), axis=-1, keepdims=True)
        position = tok * 512 + k * 128 + lax.broadcasted_iota(jnp.int32, square, 0)
        inside = jnp.where(position < limit, 1.0, 0.0)
        keep_v[k // 2, k % 2] = (kept * inside).reshape(2, 2, 2, PAGE, HD)
        move_v[k // 2, k % 2] = ((1.0 - kept) * inside).reshape(2, 2, 2, PAGE, HD)

    slots = pl.ds(pl.multiple_of(tok * PAGE, PAGE), PAGE)
    here = out_ref.at[0, :, pl.ds(layer * 2, 2), :, slots, :]

    def start(o, there):
        data = buf.at[there[1] * 4 + there[0]]
        if any(o):
            pltpu.make_async_remote_copy(
                src_ref=data, dst_ref=here, send_sem=send_sem, recv_sem=recv_sem,
                device_id=there, device_id_type=MESH,
            ).start()
        else:
            pltpu.make_async_copy(data, here, own_sem).start()

    def send(chunk):
        for o in sends_of(chunk):
            start(o, to(o))

    def send_last(chunk):
        px, py, pz = chunk
        for half, dc, sx, sy in itertools.product((0, 2), (0, 1), (0, 2), (0, 2)):
            dx, dy = px + sx, py + sy
            slot_z = lax.rem(z + pz, 2) + half
            start(chunk, (to_layer[dx][dc], slot_z * 8 + to_xy[dx][dy]))

    for k, chunk in enumerate(CHUNKS):
        loads[k].wait()
        merge(in_v, keep_v, move_v, buf, k, at(chunk))
        if k == 0:
            pl.semaphore_wait(barrier, len(everyone))
            send(chunk)
        if k > 1:
            send(CHUNKS[k - 1])
    send_last(CHUNKS[-1])

    pltpu.make_async_copy(buf.at[tok * 4 + layer], here, own_sem).wait()
    rest = buf.at[pl.ds(0, 127)]
    pltpu.make_async_copy(rest, rest, send_sem).wait()
    pltpu.make_async_copy(rest, rest, recv_sem).wait()


def put_out(in_ref, out_ref, sem):
    copies = []
    for h, j in itertools.product(range(2), range(8)):
        copies.append(pltpu.make_async_copy(in_ref.at[0, h, j], out_ref.at[0, h, j], sem.at[h * 8 + j]))
    for copy in copies:
        copy.start()
    for copy in copies:
        copy.wait()


def shards(kv_cache, keep_mask, lengths):
    landed = pl.pallas_call(
        kernel,
        out_shape=pltpu.VMEM((1, 2, 8, 2, 512, HD), jnp.bfloat16),
        in_specs=[
            pl.BlockSpec(memory_space=pltpu.SMEM),
            pl.BlockSpec(memory_space=pltpu.HBM),
            pl.BlockSpec(memory_space=pltpu.HBM),
        ],
        out_specs=pl.BlockSpec(memory_space=pltpu.VMEM),
        scratch_shapes=[
            pltpu.VMEM((1, 512), jnp.int32),
            pltpu.VMEM((8, 2, 2, 2, 2, PAGE, KVH * HD), jnp.bfloat16),
            pltpu.VMEM((2, 2, 2, 2, 2, PAGE, HD), jnp.float32),
            pltpu.VMEM((2, 2, 2, 2, 2, PAGE, HD), jnp.float32),
            pltpu.VMEM((128, 2, 2, 2, PAGE, HD), jnp.bfloat16),
            pltpu.SemaphoreType.DMA((10,)),
            pltpu.SemaphoreType.DMA,
            pltpu.SemaphoreType.DMA,
            pltpu.SemaphoreType.DMA,
        ],
        compiler_params=pltpu.CompilerParams(collective_id=0, has_side_effects=True, vmem_limit_bytes=58 << 20),
    )(lengths, keep_mask.reshape(1, 512), kv_cache.reshape(2, 2, 2, 2, 2, 2, 2, PAGE, KVH * HD))
    return pl.pallas_call(
        put_out,
        out_shape=jax.ShapeDtypeStruct((1, 2, 8, 2, 512, HD), jnp.bfloat16),
        in_specs=[pl.BlockSpec(memory_space=pltpu.VMEM)],
        out_specs=pl.BlockSpec(memory_space=pl.ANY),
        scratch_shapes=[pltpu.SemaphoreType.DMA((16,))],
        compiler_params=pltpu.CompilerParams(vmem_limit_bytes=16 << 20),
    )(landed)


def solution(mesh):
    in_specs = (P("layer", None, None, None, "tok", None), P("layer", None, "tok"), P())
    out_specs = P(None, "layer", None, None, "tok", None)
    return jax.shard_map(shards, mesh=mesh, in_specs=in_specs, out_specs=out_specs, check_vma=False)
```

```python
import functools
import itertools

import jax
import jax.numpy as jnp
from jax import lax
from jax.experimental import pallas as pl
from jax.experimental.pallas import tpu as pltpu
from jax.sharding import PartitionSpec as P

KVH = 8
HD = 128
PAGE = 16
EPS = 1e-06
MESH = pl.DeviceIdType.MESH
CHUNKS = [(1, 1, 1), (0, 0, 0), (1, 0, 0), (0, 1, 1), (0, 1, 0), (1, 0, 1), (1, 1, 0), (0, 0, 1)]


def place():
    layer = lax.axis_index("layer")
    tok = lax.axis_index("tok")
    x = (layer // 2) * 2 + (tok // 4) % 2
    return layer, tok, x, tok % 4, tok // 8, layer % 2


def hops(o):
    return sum(min(v, 4 - v) for v in o[:3])


def sends_of(chunk):
    px, py, pz = chunk
    out = []
    for dc in (0, 1):
        for sy, sz in ((0, 0), (2, 2), (2, 0), (0, 2)):
            o = (px, py + sy, pz + sz)
            n = (px + 2, (py + 2 - sy) if py else py + sy, (pz + 2 - sz) if pz else pz + sz)
            out += [o + (dc,), n + (dc,)]
    assert len(set(out)) == 16
    return out


def merge(in_v, keep_v, move_v, buf, k, at):
    zl, xl, yl = at
    def body(step, carry):
        h, c = step // 2, step % 2
        cols = pl.ds(pl.multiple_of(h * HD, HD), HD)
        a = in_v[k, 0, c, :, :, :, cols].reshape(64, HD).astype(jnp.float32)
        b = in_v[k, 1, c, :, :, :, cols].reshape(64, HD).astype(jnp.float32)
        keep = keep_v[:, zl, xl, :, yl].reshape(64, HD)
        move = move_v[:, zl, xl, :, yl].reshape(64, HD)
        ma = jnp.sum(a * a, axis=-1, keepdims=True) * (1.0 / HD) + EPS
        mb = jnp.sum(b * b, axis=-1, keepdims=True) * (1.0 / HD) + EPS
        ia, ib = lax.rsqrt(ma), lax.rsqrt(mb)
        u = a * ia + b * ib
        mu = jnp.sum(u * u, axis=-1, keepdims=True) * (1.0 / HD) + EPS
        s = move * lax.rsqrt(mu)
        lower = (keep * a + (s * (ma * ia)) * u).astype(jnp.bfloat16)
        upper = (keep * b + (s * (mb * ib)) * u).astype(jnp.bfloat16)
        for zh, yh in itertools.product(range(2), range(2)):
            first = (zh * 2 + yh) * PAGE
            block = (zh * 16 + zl * 8 + xl * 4 + yh * 2 + yl) * 4 + h // 2
            buf[block, h % 2, 0, c] = lower[first : first + PAGE]
            buf[block, h % 2, 1, c] = upper[first : first + PAGE]
        return carry

    lax.fori_loop(0, 2 * KVH, body, 0, unroll=8)


def kernel(len_ref, mask_hbm, kv_ref, out_ref, mask_ref, in_v, keep_v, move_v, buf, load_sem, own_sem, send_sem, recv_sem):
    layer, tok, x, y, z, core = place()
    everyone = [o for o in itertools.product(range(4), range(4), range(4), range(2)) if any(o)]
    everyone = sorted(everyone, key=hops, reverse=True)

    xs, ys, zs = ([lax.rem(v + d, 4) for d in range(4)] for v in (x, y, z))
    cores = [core, 1 - core]
    to_layer = [[lax.div(v, 2) * 2 + c for c in cores] for v in xs]
    to_xy = [[lax.rem(v, 2) * 4 + w for w in ys] for v in xs]

    def to(o):
        dx, dy, dz, dc = o
        return to_layer[dx][dc], zs[dz] * 8 + to_xy[dx][dy]

    def at(chunk):
        px, py, pz = chunk
        return (z + pz) % 2, (x + px) % 2, (y + py) % 2

    loads = []
    for k, chunk in enumerate(CHUNKS):
        zl, xl, yl = at(chunk)
        loads.append(pltpu.make_async_copy(kv_ref.at[:, :, :, zl, xl, :, yl], in_v.at[k], load_sem.at[k]))
    get_mask = pltpu.make_async_copy(mask_hbm, mask_ref, load_sem.at[9])
    get_mask.start()
    loads[0].start()

    barrier = pltpu.get_barrier_semaphore()
    for o in everyone:
        pl.semaphore_signal(barrier, inc=1, device_id=to(o), device_id_type=MESH)
    for load in loads[1:]:
        load.start()

    get_mask.wait()
    limit = len_ref[0]
    square = (128, 128)
    diagonal = lax.broadcasted_iota(jnp.int32, square, 0) == lax.broadcasted_iota(jnp.int32, square, 1)
    for k in range(4):
        mask = jnp.broadcast_to(mask_ref[:, k * 128 : (k + 1) * 128], square)
        kept = jnp.sum(jnp.where(diagonal & (mask > 0), 1.0, 0.0), axis=-1, keepdims=True)
        position = tok * 512 + k * 128 + lax.broadcasted_iota(jnp.int32, square, 0)
        inside = jnp.where(position < limit, 1.0, 0.0)
        keep_v[k // 2, k % 2] = (kept * inside).reshape(2, 2, 2, PAGE, HD)
        move_v[k // 2, k % 2] = ((1.0 - kept) * inside).reshape(2, 2, 2, PAGE, HD)

    slots = pl.ds(pl.multiple_of(tok * PAGE, PAGE), PAGE)
    here = out_ref.at[0, :, pl.ds(layer * 2, 2), :, slots, :]

    def start(o, there):
        data = buf.at[there[1] * 4 + there[0]]
        if any(o):
            pltpu.make_async_remote_copy(
                src_ref=data, dst_ref=here, send_sem=send_sem, recv_sem=recv_sem,
                device_id=there, device_id_type=MESH,
            ).start()
        else:
            pltpu.make_async_copy(data, here, own_sem).start()

    def send(chunk):
        for o in sends_of(chunk):
            start(o, to(o))

    def send_last(chunk):
        px, py, pz = chunk
        for half, dc, sx, sy in itertools.product((0, 2), (0, 1), (0, 2), (0, 2)):
            dx, dy = px + sx, py + sy
            slot_z = lax.rem(z + pz, 2) + half
            start(chunk, (to_layer[dx][dc], slot_z * 8 + to_xy[dx][dy]))

    for k, chunk in enumerate(CHUNKS):
        loads[k].wait()
        merge(in_v, keep_v, move_v, buf, k, at(chunk))
        if k == 0:
            pl.semaphore_wait(barrier, len(everyone))
            send(chunk)
        if k > 1:
            send(CHUNKS[k - 1])
    send_last(CHUNKS[-1])

    pltpu.make_async_copy(buf.at[tok * 4 + layer], here, own_sem).wait()
    rest = buf.at[pl.ds(0, 127)]
    pltpu.make_async_copy(rest, rest, send_sem).wait()
    pltpu.make_async_copy(rest, rest, recv_sem).wait()


def put_out(in_ref, out_ref, sem):
    copies = []
    for h, j in itertools.product(range(2), range(8)):
        copies.append(pltpu.make_async_copy(in_ref.at[0, h, j], out_ref.at[0, h, j], sem.at[h * 8 + j]))
    for copy in copies:
        copy.start()
    for copy in copies:
        copy.wait()


def shards(kv_cache, keep_mask, lengths):
    landed = pl.pallas_call(
        kernel,
        out_shape=pltpu.VMEM((1, 2, 8, 2, 512, HD), jnp.bfloat16),
        in_specs=[
            pl.BlockSpec(memory_space=pltpu.SMEM),
            pl.BlockSpec(memory_space=pltpu.HBM),
            pl.BlockSpec(memory_space=pltpu.HBM),
        ],
        out_specs=pl.BlockSpec(memory_space=pltpu.VMEM),
        scratch_shapes=[
            pltpu.VMEM((1, 512), jnp.int32),
            pltpu.VMEM((8, 2, 2, 2, 2, PAGE, KVH * HD), jnp.bfloat16),
            pltpu.VMEM((2, 2, 2, 2, 2, PAGE, HD), jnp.float32),
            pltpu.VMEM((2, 2, 2, 2, 2, PAGE, HD), jnp.float32),
            pltpu.VMEM((128, 2, 2, 2, PAGE, HD), jnp.bfloat16),
            pltpu.SemaphoreType.DMA((10,)),
            pltpu.SemaphoreType.DMA,
            pltpu.SemaphoreType.DMA,
            pltpu.SemaphoreType.DMA,
        ],
        compiler_params=pltpu.CompilerParams(collective_id=0, has_side_effects=True, vmem_limit_bytes=58 << 20),
    )(lengths, keep_mask.reshape(1, 512), kv_cache.reshape(2, 2, 2, 2, 2, 2, 2, PAGE, KVH * HD))
    return pl.pallas_call(
        put_out,
        out_shape=jax.ShapeDtypeStruct((1, 2, 8, 2, 512, HD), jnp.bfloat16),
        in_specs=[pl.BlockSpec(memory_space=pltpu.VMEM)],
        out_specs=pl.BlockSpec(memory_space=pl.ANY),
        scratch_shapes=[pltpu.SemaphoreType.DMA((16,))],
        compiler_params=pltpu.CompilerParams(vmem_limit_bytes=16 << 20),
    )(landed)


def solution(mesh):
    in_specs = (P("layer", None, None, None, "tok", None), P("layer", None, "tok"), P())
    out_specs = P(None, "layer", None, None, "tok", None)
    return jax.shard_map(shards, mesh=mesh, in_specs=in_specs, out_specs=out_specs, check_vma=False)
```
